256 devices in a mesh: tok: 32 (over y, x, core), rep: 8 (over z).
Axes of the slice: x: 4, y: 4, z: 8, core: 2. Of those that a mesh axis runs over, the one named last changes fastest.
Arguments:
- hidden_states: bfloat16 [8, 4096, 2048], P('rep', 'tok'), may hold values from -6 to 6
- routes: int32 [8, 4096, 8], P('rep', 'tok'), may hold values from 0 to 31, all different within a row; in each aligned block of 128 rows (0 to 127, 128 to 255, ..., all dimensions but the last counted through in order) at most 36 rows name the same one
- gate_prob: float32 [8, 4096, 8], P('rep', 'tok'), may hold values from 0.03 to 0.3
- gate_up: float32 [32, 2048, 2048], P('tok', 'rep'), may hold values from -0.125 to 0.125
- down: float32 [32, 1024, 2048], P('tok', 'rep'), may hold values from -0.1875 to 0.1875
Outputs:
- mixed: bfloat16 [8, 4096, 2048], P('rep', 'tok')
The draws below stay inside these ranges and needn't reach their ends.
Inputs may be any that keep to these rules, and one draw needn't show every extreme that they name: `routes`: each row names 8 different experts. No expert is named by more than 36 rows of one device's 128 tokens, and some expert reaches 36 on some devices.
All inputs are finite; a program needn't handle non-finite values.
Results may differ from the reference program's by a relative error of at most 0.012.
Values may be sent and summed in bfloat16 or wider, within the bound.
No kernel may reach another device: no remote copies, remote signals or barrier semaphores. Data moves between devices by JAX's collectives and lax.ppermute only.
A program may use at most 128 MiB of HBM per device.

```python
import math
import jax
import jax.numpy as jnp
import numpy as np
from jax import lax

D = 2048
FF = 1024
EXPERTS = 32
TOPK = 8
TOK_DEV = 128
CAP = 36
TOKENS = 4096
SERVERS = 8
N_TOK = 32
N_REP = 8


def block_levels(stream_key, dims, split, smallest, top_value):
    factor_of = 1.0
    for axis_at, shards_of in split:
        steps = jax.random.uniform(jax.random.fold_in(jax.random.fold_in(stream_key, 6), axis_at), (shards_of,), jnp.float32, smallest / len(split), top_value / len(split))
        factor_of = factor_of * jnp.repeat(jnp.exp(steps), dims[axis_at] // shards_of).reshape((-1,) + (1,) * (len(dims) - 1 - axis_at))
    return factor_of


def routed_block(key, own, number, rows, number_of, top, limit, slope):
    order = jax.random.permutation(key, number_of)
    packed, usual = portions_of(number_of, rows * top, limit, slope, True), portions_of(number_of, rows * top, limit, slope, False)
    places = jnp.arange(number_of)

    def named(sizes, offset_by):
        used = int((sizes > 0).sum())
        fixed = max(1, used // 4)
        passed = fixed + (places - fixed + offset_by * (used - fixed)) % max(1, number_of - fixed)
        return jnp.zeros((number_of,), jnp.int32).at[order[jnp.where(places < fixed, places, passed)]].set(jnp.asarray(sizes, jnp.int32))

    sizes = jnp.where(number % 4 == 0, named(packed, number // 4), named(usual, number - number // 4 - 1))
    mixed = jax.random.permutation(jax.random.fold_in(own, 3), number_of)
    giver, receiver = mixed[0:number_of // 2 * 2:2], mixed[1:number_of // 2 * 2:2]
    margin = jnp.minimum(sizes[giver] - 1, limit - sizes[receiver]) // 2
    margin = jnp.where((giver == order[0]) | (receiver == order[0]) | (sizes[receiver] == 0), 0, jnp.maximum(margin, 0))
    passed = jax.random.randint(jax.random.fold_in(own, 4), (number_of // 2,), 0, 1 << 20) % (margin + 1)
    sizes = sizes.at[giver].add(-passed).at[receiver].add(passed)
    labels = jnp.searchsorted(jnp.cumsum(sizes), jnp.arange(rows * top), side="right").astype(jnp.int32)
    listing = labels.reshape(top, rows).T
    listing = listing[jax.random.permutation(jax.random.fold_in(own, 1), rows)]
    offset_by = jax.random.randint(jax.random.fold_in(own, 2), (rows, 1), 0, top)
    return jnp.take_along_axis(listing, (jnp.arange(top)[None, :] + offset_by) % top, axis=1)


def portions_of(amount, total, bound, slope, full):
    portions = [(1 << 20) // math.isqrt(standing ** slope) + 1 for standing in range(1, amount + 1)]
    largest = bound if full else min(bound, max(-(-total // amount), total * portions[0] // sum(portions)))
    least = 1 if total - largest >= amount - 1 else 0
    given, spare = [largest] + [least] * (amount - 1), total - largest - least * (amount - 1)
    while spare > 0:
        movable = [i for i in range(1, amount) if given[i] < largest] or [i for i in range(1, amount) if given[i] < bound]
        mass, budget = sum([portions[i] for i in movable]), spare
        for i in movable:
            more = min(bound - given[i], max(1, budget * portions[i] // mass), spare)
            given[i] = given[i] + more
            spare = spare - more
    return np.array(given)


def noise(stream_key, extent, scale, bound, shards=(), kind=jnp.bfloat16):
    array = scale * jax.random.normal(stream_key, extent, jnp.float32)
    if shards:
        array = array * block_levels(stream_key, extent, shards, -0.22, 0.18)
    return jnp.clip(array, -bound, bound).astype(kind)


def setup_inputs(seed: int = 0) -> dict:
    seeds = jax.random.split(jax.random.key(seed), 6)
    hidden_states = noise(seeds[0], (SERVERS, TOKENS, D), 1.0, 6.0, ((0, 8), (1, 32)))
    routes_keys = jax.random.split(jax.random.fold_in(seeds[1], 1), SERVERS * TOKENS // TOK_DEV)
    routes_turns = jax.random.permutation(jax.random.fold_in(seeds[1], 3), SERVERS * TOKENS // TOK_DEV)
    routes = jax.vmap(lambda own, number: routed_block(jax.random.fold_in(seeds[1], 2), own, number, TOK_DEV, EXPERTS, TOPK, CAP, 1))(routes_keys, routes_turns).reshape((SERVERS, TOKENS, TOPK))
    gate_prob = jnp.clip(jnp.exp(math.log(0.3) - 2.3025852 * jax.random.uniform(seeds[2], (SERVERS, TOKENS, TOPK), jnp.float32) ** block_levels(seeds[2], (SERVERS, TOKENS, TOPK), ((0, 8), (1, 32)), -0.2, 0.2)), 0.03, 0.3)
    gate_up = noise(seeds[3], (EXPERTS, D, 2 * FF), D ** -0.5, 0.125, ((0, 32), (1, 8)), jnp.float32)
    down = noise(seeds[4], (EXPERTS, FF, D), FF ** -0.5, 0.1875, ((0, 32), (1, 8)), jnp.float32)
    return dict(hidden_states=hidden_states, routes=routes, gate_prob=gate_prob, gate_up=gate_up, down=down)


def reference(hidden_states, routes, gate_prob, gate_up, down):
    served_gate_up = gate_up.astype(jnp.bfloat16)
    served_down = down.astype(jnp.bfloat16)
    flat_rows = hidden_states.reshape(-1, D)
    flat_picks = routes.reshape(-1).astype(jnp.int32)
    flat_probs = gate_prob.reshape(-1)
    pick_count = flat_picks.shape[0]
    owners = (jnp.arange(pick_count, dtype=jnp.int32) // TOPK).astype(jnp.int32)
    most_rows = N_REP * N_TOK * CAP

    def one_expert(running, expert):
        chosen = jnp.nonzero(flat_picks == expert, size=most_rows, fill_value=pick_count)[0].astype(jnp.int32)
        usable = chosen < pick_count
        safe_index = jnp.where(usable, chosen, 0).astype(jnp.int32)
        token_index = owners[safe_index]
        rows = flat_rows[token_index]
        both_parts = jnp.dot(rows, served_gate_up[expert], preferred_element_type=jnp.float32)
        units = (jax.nn.silu(both_parts[:, :FF]) * both_parts[:, FF:]).astype(jnp.bfloat16)
        expert_out = jnp.dot(units, served_down[expert], preferred_element_type=jnp.float32).astype(jnp.bfloat16)
        weights = jnp.where(usable, flat_probs[safe_index], jnp.float32(0.0))
        weighted = expert_out.astype(jnp.float32) * weights[:, None]
        running = running.at[token_index].add(weighted)
        return running, None

    start_sum = jnp.zeros((flat_rows.shape[0], D), jnp.float32)
    total, unused_out = lax.scan(one_expert, start_sum, jnp.arange(EXPERTS, dtype=jnp.int32))
    return total.astype(jnp.bfloat16).reshape(hidden_states.shape)
```

```python
import functools

import jax
import jax.numpy as jnp
from jax import lax
from jax.experimental import pallas as pl
from jax.experimental.pallas import tpu as pltpu
from jax.sharding import PartitionSpec as P

CAP = 36
PAD = 40
MAIN = 32
NONE = 200.0
GATE_CHUNKS = 2
DOWN_WIDTHS = (512, 512, 512, 512)


def slots_of(picks, experts):
    count, tokens = experts.shape[0], picks.shape[1]
    named = jnp.zeros((count, tokens), jnp.float32)
    for k in range(picks.shape[0]):
        named = named + (picks[k : k + 1, :] == experts).astype(jnp.float32)
    before = lax.broadcasted_iota(jnp.int32, (tokens, tokens), 0)
    after = lax.broadcasted_iota(jnp.int32, (tokens, tokens), 1)
    earlier = (before < after).astype(jnp.bfloat16)
    slot = jnp.dot(named.astype(jnp.bfloat16), earlier, preferred_element_type=jnp.float32)
    return jnp.where(named > 0.0, slot, NONE)


def dispatch_kernel(picks_ref, rows_ref, send_ref):
    tokens = picks_ref.shape[1]
    group = send_ref.shape[0] // PAD
    experts = pl.program_id(0) * group + lax.broadcasted_iota(jnp.int32, (group, tokens), 0)
    slot = slots_of(picks_ref[...], experts)
    place = lax.broadcasted_iota(jnp.int32, (group, PAD, tokens), 1).astype(jnp.float32)
    chosen = (slot[:, None, :] == place).astype(jnp.float32)
    chosen = chosen.reshape(group * PAD, tokens).astype(jnp.bfloat16)
    send_ref[...] = jnp.dot(chosen, rows_ref[...], preferred_element_type=jnp.float32).astype(
        jnp.bfloat16
    )


def dispatch(picks, rows, all_experts):
    top, tokens = picks.shape
    width = rows.shape[1]
    group = 8
    return pl.pallas_call(
        dispatch_kernel,
        out_shape=jax.ShapeDtypeStruct((all_experts * PAD, width), jnp.bfloat16),
        grid=(all_experts // group,),
        in_specs=[
            pl.BlockSpec((top, tokens), lambda i: (0, 0)),
            pl.BlockSpec((tokens, width), lambda i: (0, 0)),
        ],
        out_specs=pl.BlockSpec((group * PAD, width), lambda i: (i, 0)),
        cost_estimate=pl.CostEstimate(
            flops=2 * all_experts * PAD * tokens * width,
            bytes_accessed=2 * width * (tokens + all_experts * PAD),
            transcendentals=0,
        ),
        name="dispatch",
    )(picks, rows)


def mixer_kernel(picks_ref, probs_ref, high_ref, low_ref):
    tokens = picks_ref.shape[1]
    group = high_ref.shape[0] // 72
    experts = pl.program_id(0) * group + lax.broadcasted_iota(jnp.int32, (group, tokens), 0)
    slot = slots_of(picks_ref[...], experts)
    weight = jnp.zeros((group, tokens), jnp.float32)
    for k in range(picks_ref.shape[0]):
        weight = weight + jnp.where(
            picks_ref[k : k + 1, :] == experts, probs_ref[k : k + 1, :], 0.0
        )
    low_half = jnp.where(slot < MAIN, slot, slot + MAIN)
    high_half = jnp.where(slot < MAIN, slot + MAIN, slot + MAIN + CAP - MAIN)
    row = jnp.concatenate([low_half, high_half], axis=1)
    weight = jnp.concatenate([weight, weight], axis=1)
    place = lax.broadcasted_iota(jnp.int32, (group, 72, 2 * tokens), 1).astype(jnp.float32)
    spread = jnp.where(row[:, None, :] == place, weight[:, None, :], 0.0)
    spread = spread.reshape(group * 72, 2 * tokens)
    high = spread.astype(jnp.bfloat16)
    high_ref[...] = high
    low_ref[...] = (spread - high.astype(jnp.float32)).astype(jnp.bfloat16)


def mixer(picks, probs, all_experts):
    top, tokens = picks.shape
    group = 8
    shape = jax.ShapeDtypeStruct((all_experts * 72, 2 * tokens), jnp.bfloat16)
    return pl.pallas_call(
        mixer_kernel,
        out_shape=(shape, shape),
        grid=(all_experts // group,),
        in_specs=[
            pl.BlockSpec((top, tokens), lambda i: (0, 0)),
            pl.BlockSpec((top, tokens), lambda i: (0, 0)),
        ],
        out_specs=(
            pl.BlockSpec((group * 72, 2 * tokens), lambda i: (i, 0)),
            pl.BlockSpec((group * 72, 2 * tokens), lambda i: (i, 0)),
        ),
        cost_estimate=pl.CostEstimate(
            flops=all_experts * 72 * 2 * tokens * 4,
            bytes_accessed=8 * all_experts * 72 * tokens,
            transcendentals=0,
        ),
        name="mixer",
    )(picks, probs)


def load_pieces(order_ref, piece_refs, whole, sem):
    rows = piece_refs[0].shape[0]
    copies = []
    for i, piece in enumerate(piece_refs):
        start = pl.multiple_of(order_ref[i] * rows, rows)
        copies.append(pltpu.make_async_copy(piece, whole.at[pl.ds(start, rows), :], sem.at[i]))
    for copy in copies:
        copy.start()
    for copy in copies:
        copy.wait()


def gate_kernel(pieces, order_ref, rows_ref, *refs):
    piece_refs, (unit_ref, whole, sem) = refs[:pieces], refs[pieces:]

    @pl.when(pl.program_id(0) == 0)
    def _():
        load_pieces(order_ref, piece_refs, whole, sem)

    both = jnp.dot(rows_ref[...], whole[...], preferred_element_type=jnp.float32)
    half = both.shape[1] // 2
    gate, up = both[:, :half], both[:, half:]
    unit_ref[...] = (gate / (1.0 + jnp.exp(-gate)) * up).astype(jnp.bfloat16)


def gate_units(order, rows, pieces):
    count, width = rows.shape
    depth, columns = pieces[0].shape
    block = 320
    return pl.pallas_call(
        functools.partial(gate_kernel, len(pieces)),
        out_shape=jax.ShapeDtypeStruct((count, columns // 2), jnp.bfloat16),
        grid_spec=pltpu.PrefetchScalarGridSpec(
            num_scalar_prefetch=1,
            grid=(count // block,),
            in_specs=[pl.BlockSpec((block, width), lambda i, order: (i, 0))]
            + [pl.BlockSpec(memory_space=pl.ANY)] * len(pieces),
            out_specs=pl.BlockSpec((block, columns // 2), lambda i, order: (i, 0)),
            scratch_shapes=[
                pltpu.VMEM((depth * len(pieces), columns), jnp.bfloat16),
                pltpu.SemaphoreType.DMA((len(pieces),)),
            ],
        ),
        compiler_params=pltpu.CompilerParams(vmem_limit_bytes=40 << 20),
        cost_estimate=pl.CostEstimate(
            flops=2 * count * width * columns,
            bytes_accessed=2 * (count * width + width * columns + count * columns // 2),
            transcendentals=count * columns // 2,
        ),
        name="gate_units",
    )(order, rows, *pieces)


def down_kernel(pieces, unit_count, order_ref, *refs):
    unit_refs, refs = refs[:unit_count], refs[unit_count:]
    piece_refs, (out_ref, whole, sem) = refs[:pieces], refs[pieces:]

    @pl.when(pl.program_id(0) == 0)
    def _():
        load_pieces(order_ref, piece_refs, whole, sem)

    depth = unit_refs[0].shape[1]
    total = None
    for i, unit in enumerate(unit_refs):
        part = jnp.dot(
            unit[...], whole[i * depth : (i + 1) * depth, :], preferred_element_type=jnp.float32
        )
        total = part if total is None else total + part
    half = total.shape[1] // 2
    group = total.shape[0] // PAD
    total = total.reshape(group, PAD, 2 * half)
    left, right = total[:, :, :half], total[:, :, half:]
    last = left[:, MAIN:, :] + pltpu.roll(right[:, MAIN:, :], 4, 1)
    packed = jnp.concatenate([left[:, :MAIN, :], right[:, :MAIN, :], last], axis=1)
    out_ref[...] = packed.reshape(group * 72, half).astype(jnp.bfloat16)


def down_rows(order, units, pieces):
    count = units[0].shape[0]
    depth, columns = pieces[0].shape
    group = 8
    return pl.pallas_call(
        functools.partial(down_kernel, len(pieces), len(units)),
        out_shape=jax.ShapeDtypeStruct((count // PAD * 72, columns // 2), jnp.bfloat16),
        grid_spec=pltpu.PrefetchScalarGridSpec(
            num_scalar_prefetch=1,
            grid=(count // PAD // group,),
            in_specs=[
                pl.BlockSpec((group * PAD, unit.shape[1]), lambda i, order: (i, 0))
                for unit in units
            ]
            + [pl.BlockSpec(memory_space=pl.ANY)] * len(pieces),
            out_specs=pl.BlockSpec((group * 72, columns // 2), lambda i, order: (i, 0)),
            scratch_shapes=[
                pltpu.VMEM((depth * len(pieces), columns), jnp.bfloat16),
                pltpu.SemaphoreType.DMA((len(pieces),)),
            ],
        ),
        compiler_params=pltpu.CompilerParams(vmem_limit_bytes=40 << 20),
        cost_estimate=pl.CostEstimate(
            flops=2 * count * depth * len(pieces) * columns,
            bytes_accessed=2 * (count * depth * len(pieces) + depth * len(pieces) * columns + count * columns),
            transcendentals=0,
        ),
        name="down_rows",
    )(order, *units, *pieces)


def ring_gather(piece, ranks, rightward):
    right = [(i, (i + 1) % ranks) for i in range(ranks)]
    left = [(i, (i - 1) % ranks) for i in range(ranks)]
    from_left, from_right = [piece], [piece]
    for step in range(max(rightward, ranks - 1 - rightward)):
        if step < rightward:
            from_left.append(lax.ppermute(from_left[-1], "rep", right))
        if step < ranks - 1 - rightward:
            from_right.append(lax.ppermute(from_right[-1], "rep", left))
    return from_left + from_right[1:]


def source_order(ranks, rightward):
    me = lax.axis_index("rep")
    offsets = [0] + [-s for s in range(1, rightward + 1)] + [
        s for s in range(1, ranks - rightward)
    ]
    return (me + jnp.array(offsets, jnp.int32)) % ranks


def per_device(hidden_states, routes, gate_prob, gate_up, down):
    groups = lax.axis_size("tok")
    ranks = lax.axis_size("rep")
    width = hidden_states.shape[2]
    tokens = hidden_states.shape[1]
    unit_count = gate_up.shape[2] // 2
    all_experts = groups * gate_up.shape[0]
    rightward = [(ranks - 1 + 1 - i % 2) // 2 for i in range(2)]
    orders = [source_order(ranks, r) for r in rightward]

    part = unit_count // GATE_CHUNKS
    gate_pieces = []
    for i in range(GATE_CHUNKS):
        columns = jnp.concatenate(
            [
                gate_up[0, :, i * part : (i + 1) * part],
                gate_up[0, :, unit_count + i * part : unit_count + (i + 1) * part],
            ],
            axis=1,
        )
        gate_pieces.append(ring_gather(columns.astype(jnp.bfloat16), ranks, rightward[i % 2]))

    picks, probs = routes[0].T, gate_prob[0].T
    send = dispatch(picks, hidden_states[0], all_experts)
    arrived = lax.all_to_all(
        send.reshape(groups, PAD, width), "tok", split_axis=0, concat_axis=0, tiled=True
    ).reshape(groups * PAD, width)
    high, low = mixer(picks, probs, all_experts)

    down_pieces, gate_tail = [], gate_pieces[-1][rightward[(GATE_CHUNKS - 1) % 2]]
    start = 0
    for i, columns in enumerate(DOWN_WIDTHS):
        piece = down[0, :, start : start + columns].astype(jnp.bfloat16)
        start += columns
        piece, _ = lax.optimization_barrier((piece, gate_pieces[0][2]))
        down_pieces.append(ring_gather(piece, ranks, rightward[i % 2]))

    units = [
        gate_units(orders[i % 2], arrived, pieces) for i, pieces in enumerate(gate_pieces)
    ]
    outs = []
    for i, pieces in enumerate(down_pieces):
        rows = down_rows(orders[i % 2], units, pieces)
        half = rows.shape[1]
        back = lax.all_to_all(
            rows.reshape(groups, 72, half), "tok", split_axis=0, concat_axis=0, tiled=True
        ).reshape(groups * 72, half)
        contract = (((0,), (0,)), ((), ()))
        mixed = lax.dot_general(high, back, contract, preferred_element_type=jnp.float32)
        mixed = mixed + lax.dot_general(low, back, contract, preferred_element_type=jnp.float32)
        mixed = mixed.astype(jnp.bfloat16)
        outs.extend([mixed[:tokens], mixed[tokens:]])
    return jnp.concatenate(outs, axis=1)[None]


def solution(mesh):
    return jax.shard_map(
        per_device,
        mesh=mesh,
        in_specs=(
            P("rep", "tok", None),
            P("rep", "tok", None),
            P("rep", "tok", None),
            P("tok", "rep", None),
            P("tok", "rep", None),
        ),
        out_specs=P("rep", "tok", None),
        check_vma=False,
    )
```

```python
import functools

import jax
import jax.numpy as jnp
from jax import lax
from jax.experimental import pallas as pl
from jax.experimental.pallas import tpu as pltpu
from jax.sharding import PartitionSpec as P

CAP = 36
PAD = 40
MAIN = 32
PACKED = 72
NONE = 200.0
UNIT_BLOCK = 256
EARLY = 768
RANKS = 8
VMEM_LIMIT = 56 << 20


def slots_of(picks, experts):
    count, tokens = experts.shape[0], picks.shape[1]
    named = jnp.zeros((count, tokens), jnp.float32)
    for k in range(picks.shape[0]):
        named = named + (picks[k : k + 1, :] == experts).astype(jnp.float32)
    before = lax.broadcasted_iota(jnp.int32, (tokens, tokens), 0)
    after = lax.broadcasted_iota(jnp.int32, (tokens, tokens), 1)
    earlier = (before < after).astype(jnp.bfloat16)
    slot = jnp.dot(named.astype(jnp.bfloat16), earlier, preferred_element_type=jnp.float32)
    return jnp.where(named > 0.0, slot, NONE)


def dispatch_kernel(picks_ref, rows_ref, send_ref):
    tokens = picks_ref.shape[1]
    group = send_ref.shape[0] // PAD
    experts = pl.program_id(0) * group + lax.broadcasted_iota(jnp.int32, (group, tokens), 0)
    slot = slots_of(picks_ref[...], experts)
    place = lax.broadcasted_iota(jnp.int32, (group, PAD, tokens), 1).astype(jnp.float32)
    chosen = (slot[:, None, :] == place).astype(jnp.float32)
    chosen = chosen.reshape(group * PAD, tokens).astype(jnp.bfloat16)
    send_ref[...] = jnp.dot(chosen, rows_ref[...], preferred_element_type=jnp.float32).astype(
        jnp.bfloat16
    )


def dispatch(picks, rows, all_experts):
    top, tokens = picks.shape
    width = rows.shape[1]
    group = 8
    return pl.pallas_call(
        dispatch_kernel,
        out_shape=jax.ShapeDtypeStruct((all_experts * PAD, width), jnp.bfloat16),
        grid=(all_experts // group,),
        in_specs=[
            pl.BlockSpec((top, tokens), lambda i: (0, 0)),
            pl.BlockSpec((tokens, width), lambda i: (0, 0)),
        ],
        out_specs=pl.BlockSpec((group * PAD, width), lambda i: (i, 0)),
        cost_estimate=pl.CostEstimate(
            flops=2 * all_experts * PAD * tokens * width,
            bytes_accessed=2 * width * (tokens + all_experts * PAD),
            transcendentals=0,
        ),
        name="dispatch",
    )(picks, rows)


def mixer_kernel(picks_ref, probs_ref, mix_ref):
    tokens = picks_ref.shape[1]
    group = mix_ref.shape[1] // PACKED
    experts = pl.program_id(0) * group + lax.broadcasted_iota(jnp.int32, (group, tokens), 0)
    slot = slots_of(picks_ref[...], experts)
    weight = jnp.zeros((group, tokens), jnp.float32)
    for k in range(picks_ref.shape[0]):
        weight = weight + jnp.where(
            picks_ref[k : k + 1, :] == experts, probs_ref[k : k + 1, :], 0.0
        )
    first = jnp.where(slot < MAIN, slot, slot + MAIN)
    second = jnp.where(slot < MAIN, slot + MAIN, slot + CAP)
    row = jnp.concatenate([first, second], axis=1)
    weight = jnp.concatenate([weight, weight], axis=1)
    place = lax.broadcasted_iota(jnp.int32, (group, PACKED, 2 * tokens), 1).astype(jnp.float32)
    spread = jnp.where(row[:, None, :] == place, weight[:, None, :], 0.0)
    spread = spread.reshape(group * PACKED, 2 * tokens).T
    high = spread.astype(jnp.bfloat16)
    mix_ref[: 2 * tokens, :] = high
    mix_ref[2 * tokens :, :] = (spread - high.astype(jnp.float32)).astype(jnp.bfloat16)


def mixer(picks, probs, all_experts):
    top, tokens = picks.shape
    group = 16
    return pl.pallas_call(
        mixer_kernel,
        out_shape=jax.ShapeDtypeStruct((4 * tokens, all_experts * PACKED), jnp.bfloat16),
        grid=(all_experts // group,),
        in_specs=[
            pl.BlockSpec((top, tokens), lambda i: (0, 0)),
            pl.BlockSpec((top, tokens), lambda i: (0, 0)),
        ],
        out_specs=pl.BlockSpec((4 * tokens, group * PACKED), lambda i: (0, i)),
        compiler_params=pltpu.CompilerParams(vmem_limit_bytes=24 << 20),
        cost_estimate=pl.CostEstimate(
            flops=all_experts * PACKED * 2 * tokens * 8,
            bytes_accessed=8 * all_experts * PACKED * tokens,
            transcendentals=0,
        ),
        name="mixer",
    )(picks, probs)


def mix_kernel(mix_ref, back_ref, *refs):
    out_ref = refs[-1]
    tokens = out_ref.shape[0]
    start = refs[0].shape[1] if len(refs) > 1 else 0
    half = back_ref.shape[1]
    both = jnp.dot(mix_ref[...], back_ref[...], preferred_element_type=jnp.float32)
    total = (both[: 2 * tokens] + both[2 * tokens :]).astype(jnp.bfloat16)
    if start:
        out_ref[:, :start] = refs[0][...]
    out_ref[:, start : start + half] = total[:tokens]
    out_ref[:, start + half :] = total[tokens:]


def mix_rows(mix, back, *ready):
    tokens = mix.shape[0] // 4
    width = 2 * back.shape[1] + sum(part.shape[1] for part in ready)
    operands = (mix, back, *ready)
    return pl.pallas_call(
        mix_kernel,
        out_shape=jax.ShapeDtypeStruct((tokens, width), jnp.bfloat16),
        grid=(1,),
        in_specs=[pl.BlockSpec(part.shape, lambda i: (0, 0)) for part in operands],
        out_specs=pl.BlockSpec((tokens, width), lambda i: (0, 0)),
        compiler_params=pltpu.CompilerParams(vmem_limit_bytes=24 << 20),
        cost_estimate=pl.CostEstimate(
            flops=2 * mix.shape[0] * mix.shape[1] * back.shape[1],
            bytes_accessed=2 * (mix.size + back.size + tokens * width),
            transcendentals=0,
        ),
        name="mix",
    )(*operands)


def cast_kernel(gate_ref, down_ref, out_ref):
    width, half = gate_ref.shape[1], out_ref.shape[1] - gate_ref.shape[1]
    rows = down_ref.shape[0]
    out_ref[:, :width] = gate_ref[...].astype(jnp.bfloat16)
    out_ref[:rows, width:] = down_ref[:, :half].astype(jnp.bfloat16)
    out_ref[rows:, width:] = down_ref[:, half:].astype(jnp.bfloat16)


def cast_first(gate_up, down, early):
    rows, width = gate_up.shape
    return pl.pallas_call(
        cast_kernel,
        out_shape=jax.ShapeDtypeStruct((rows, width + early // 2), jnp.bfloat16),
        grid=(1,),
        in_specs=[
            pl.BlockSpec((rows, width), lambda i: (0, 0)),
            pl.BlockSpec((rows // 2, early), lambda i: (0, 0)),
        ],
        out_specs=pl.BlockSpec((rows, width + early // 2), lambda i: (0, 0)),
        compiler_params=pltpu.CompilerParams(vmem_limit_bytes=VMEM_LIMIT),
        name="cast_first",
    )(gate_up, down)


def packed_rows(left, right):
    group, half = left.shape[0] // PAD, left.shape[1]
    left, right = left.reshape(group, PAD, half), right.reshape(group, PAD, half)
    last = left[:, MAIN:, :] + pltpu.roll(right[:, MAIN:, :], PAD - CAP, 1)
    packed = jnp.concatenate([left[:, :MAIN, :], right[:, :MAIN, :], last], axis=1)
    return packed.reshape(group * PACKED, half).astype(jnp.bfloat16)


def front_kernel(
    blocks, rows_ref, gate_ref, up_ref, weight_ref, unit_ref, out_ref, units, early, sem
):
    step = pl.program_id(0)
    width = weight_ref.shape[1] - early.shape[1]
    copy = pltpu.make_async_copy(weight_ref.at[:, width:], early, sem)

    @pl.when(step == 0)
    def _():
        copy.start()

    @pl.when(step < blocks)
    def _():
        gate = jnp.dot(rows_ref[...], gate_ref[...], preferred_element_type=jnp.float32)
        up = jnp.dot(rows_ref[...], up_ref[...], preferred_element_type=jnp.float32)
        unit = (gate * (0.5 * jnp.tanh(0.5 * gate) + 0.5) * up).astype(jnp.bfloat16)
        unit_ref[...] = unit
        units[:, pl.ds(pl.multiple_of(step * UNIT_BLOCK, UNIT_BLOCK), UNIT_BLOCK)] = unit

    @pl.when(step == blocks)
    def _():
        copy.wait()

    @pl.when(step >= blocks)
    def _():
        count = out_ref.shape[0] // PACKED * PAD
        block = units[pl.ds(pl.multiple_of((step - blocks) * count, count), count), :]
        depth = block.shape[1] // RANKS
        parts = []
        for half in range(2):
            weight = jnp.concatenate(
                [
                    early[(2 * rank + half) * depth : (2 * rank + half + 1) * depth, :]
                    for rank in range(RANKS)
                ],
                axis=0,
            )
            parts.append(jnp.dot(block, weight, preferred_element_type=jnp.float32))
        out_ref[...] = packed_rows(*parts)


def front(rows, weight, unit_count):
    count, width = rows.shape
    half = weight.shape[1] - 2 * unit_count
    blocks, group = unit_count // UNIT_BLOCK, 8
    last = blocks - 1
    return pl.pallas_call(
        functools.partial(front_kernel, blocks),
        out_shape=(
            jax.ShapeDtypeStruct((count, unit_count), jnp.bfloat16),
            jax.ShapeDtypeStruct((count // PAD * PACKED, half), jnp.bfloat16),
        ),
        grid=(blocks + count // PAD // group,),
        in_specs=[
            pl.BlockSpec((count, width), lambda i: (0, 0), pipeline_mode=pl.Buffered(1)),
            pl.BlockSpec((width, UNIT_BLOCK), lambda i: (0, jnp.minimum(i, last))),
            pl.BlockSpec((width, UNIT_BLOCK), lambda i: (0, blocks + jnp.minimum(i, last))),
            pl.BlockSpec(memory_space=pl.ANY),
        ],
        out_specs=(
            pl.BlockSpec((count, UNIT_BLOCK), lambda i: (0, jnp.minimum(i, last))),
            pl.BlockSpec((group * PACKED, half), lambda i: (jnp.maximum(i - blocks, 0), 0)),
        ),
        scratch_shapes=[
            pltpu.VMEM((count, unit_count), jnp.bfloat16),
            pltpu.VMEM((weight.shape[0], half), jnp.bfloat16),
            pltpu.SemaphoreType.DMA,
        ],
        compiler_params=pltpu.CompilerParams(vmem_limit_bytes=VMEM_LIMIT),
        cost_estimate=pl.CostEstimate(
            flops=4 * count * width * unit_count + 4 * count * unit_count * half,
            bytes_accessed=2 * (count * width + weight.size + count * unit_count),
            transcendentals=count * unit_count,
        ),
        name="front",
    )(rows, weight, weight, weight)


def down_kernel(unit_ref, weight_ref, out_ref):
    total = jnp.dot(unit_ref[...], weight_ref[...], preferred_element_type=jnp.float32)
    half = total.shape[1] // 2
    out_ref[...] = packed_rows(total[:, :half], total[:, half:])


def down_rows(units, weight):
    count, depth = units.shape
    group, half = 8, weight.shape[1] // 2
    return pl.pallas_call(
        down_kernel,
        out_shape=jax.ShapeDtypeStruct((count // PAD * PACKED, half), jnp.bfloat16),
        grid=(count // PAD // group,),
        in_specs=[
            pl.BlockSpec((group * PAD, depth), lambda i: (i, 0)),
            pl.BlockSpec(weight.shape, lambda i: (0, 0), pipeline_mode=pl.Buffered(1)),
        ],
        out_specs=pl.BlockSpec((group * PACKED, half), lambda i: (i, 0)),
        compiler_params=pltpu.CompilerParams(vmem_limit_bytes=VMEM_LIMIT),
        cost_estimate=pl.CostEstimate(
            flops=4 * count * depth * half,
            bytes_accessed=2 * depth * (count + 2 * half) + 4 * count * half,
            transcendentals=0,
        ),
        name="down_rows",
    )(units, weight)


def per_device(hidden_states, routes, gate_prob, gate_up, down):
    groups = lax.axis_size("tok")
    width = hidden_states.shape[2]
    unit_count = gate_up.shape[2] // 2
    all_experts = groups * gate_up.shape[0]
    gate_up, down = gate_up[0], down[0]

    first = lax.all_gather(cast_first(gate_up, down, EARLY), "rep", axis=0, tiled=True)
    rest = lax.all_gather(
        down[:, EARLY:].astype(jnp.bfloat16), "rep", axis=0, tiled=True
    )

    picks, probs = routes[0].T, gate_prob[0].T
    send = dispatch(picks, hidden_states[0], all_experts)
    arrived = lax.all_to_all(
        send.reshape(groups, PAD, width), "tok", split_axis=0, concat_axis=0, tiled=True
    ).reshape(groups * PAD, width)
    mix = mixer(picks, probs, all_experts)

    units, sent = front(arrived, first, unit_count)
    ready = ()
    for part in range(2):
        if part:
            sent = down_rows(units, rest)
        half = sent.shape[1]
        back = lax.all_to_all(
            sent.reshape(groups, PACKED, half), "tok", split_axis=0, concat_axis=0, tiled=True
        ).reshape(groups * PACKED, half)
        ready = (mix_rows(mix, back, *ready),)
    return ready[0][None]


def solution(mesh):
    return jax.shard_map(
        per_device,
        mesh=mesh,
        in_specs=(
            P("rep", "tok", None),
            P("rep", "tok", None),
            P("rep", "tok", None),
            P("tok", "rep", None),
            P("tok", "rep", None),
        ),
        out_specs=P("rep", "tok", None),
        check_vma=False,
    )
```

```python
import functools

import jax
import jax.numpy as jnp
from jax import lax
from jax.experimental import pallas as pl
from jax.experimental.pallas import tpu as pltpu
from jax.sharding import PartitionSpec as P

CAP = 36
PAD = 40
MAIN = 32
PACKED = 72
NONE = 200.0
EARLY = 1024
WINDOW = 3
MIXER_FLOPS = 40 * 10**9
ORDER = ("ABABABA", "ABABABB")
LATE_ORDER = ("efefefe", "efefeff")
VMEM_LIMIT = 56 << 20


def slots_of(picks, experts):
    count, tokens = experts.shape[0], picks.shape[1]
    named = jnp.zeros((count, tokens), jnp.float32)
    for k in range(picks.shape[0]):
        named = named + (picks[k : k + 1, :] == experts).astype(jnp.float32)
    before = lax.broadcasted_iota(jnp.int32, (tokens, tokens), 0)
    after = lax.broadcasted_iota(jnp.int32, (tokens, tokens), 1)
    earlier = (before < after).astype(jnp.bfloat16)
    slot = jnp.dot(named.astype(jnp.bfloat16), earlier, preferred_element_type=jnp.float32)
    return jnp.where(named > 0.0, slot, NONE)


def dispatch_kernel(picks_ref, rows_ref, send_ref):
    tokens = picks_ref.shape[1]
    group = send_ref.shape[0] // PAD
    experts = pl.program_id(0) * group + lax.broadcasted_iota(jnp.int32, (group, tokens), 0)
    slot = slots_of(picks_ref[...], experts)
    place = lax.broadcasted_iota(jnp.int32, (group, PAD, tokens), 1).astype(jnp.float32)
    chosen = (slot[:, None, :] == place).astype(jnp.float32)
    chosen = chosen.reshape(group * PAD, tokens).astype(jnp.bfloat16)
    send_ref[...] = jnp.dot(chosen, rows_ref[...], preferred_element_type=jnp.float32).astype(
        jnp.bfloat16
    )


def dispatch(picks, rows, all_experts):
    top, tokens = picks.shape
    width = rows.shape[1]
    group = 16
    return pl.pallas_call(
        dispatch_kernel,
        out_shape=jax.ShapeDtypeStruct((all_experts * PAD, width), jnp.bfloat16),
        grid=(all_experts // group,),
        in_specs=[
            pl.BlockSpec((top, tokens), lambda i: (0, 0)),
            pl.BlockSpec((tokens, width), lambda i: (0, 0)),
        ],
        out_specs=pl.BlockSpec((group * PAD, width), lambda i: (i, 0)),
        cost_estimate=pl.CostEstimate(
            flops=2 * all_experts * PAD * tokens * width,
            bytes_accessed=2 * width * (tokens + all_experts * PAD),
            transcendentals=0,
        ),
        compiler_params=pltpu.CompilerParams(vmem_limit_bytes=VMEM_LIMIT),
        name="dispatch",
    )(picks, rows)


def mixer_kernel(picks_ref, probs_ref, mix_ref):
    tokens = picks_ref.shape[1]
    group = mix_ref.shape[1] // PACKED
    experts = pl.program_id(0) * group + lax.broadcasted_iota(jnp.int32, (group, tokens), 0)
    slot = slots_of(picks_ref[...], experts)
    weight = jnp.zeros((group, tokens), jnp.float32)
    for k in range(picks_ref.shape[0]):
        weight = weight + jnp.where(
            picks_ref[k : k + 1, :] == experts, probs_ref[k : k + 1, :], 0.0
        )
    first = jnp.where(slot < MAIN, slot, slot + MAIN)
    second = jnp.where(slot < MAIN, slot + MAIN, slot + CAP)
    row = jnp.concatenate([first, second], axis=1)
    weight = jnp.concatenate([weight, weight], axis=1)
    place = lax.broadcasted_iota(jnp.int32, (group, PACKED, 2 * tokens), 1).astype(jnp.float32)
    spread = jnp.where(row[:, None, :] == place, weight[:, None, :], 0.0)
    spread = spread.reshape(group * PACKED, 2 * tokens).T
    high = spread.astype(jnp.bfloat16)
    mix_ref[: 2 * tokens, :] = high
    mix_ref[2 * tokens :, :] = (spread - high.astype(jnp.float32)).astype(jnp.bfloat16)


def mixer(picks, probs, all_experts):
    top, tokens = picks.shape
    group = 16
    return pl.pallas_call(
        mixer_kernel,
        out_shape=jax.ShapeDtypeStruct((4 * tokens, all_experts * PACKED), jnp.bfloat16),
        grid=(all_experts // group,),
        in_specs=[
            pl.BlockSpec((top, tokens), lambda i: (0, 0)),
            pl.BlockSpec((top, tokens), lambda i: (0, 0)),
        ],
        out_specs=pl.BlockSpec((4 * tokens, group * PACKED), lambda i: (0, i)),
        compiler_params=pltpu.CompilerParams(vmem_limit_bytes=32 << 20),
        cost_estimate=pl.CostEstimate(
            flops=MIXER_FLOPS,
            bytes_accessed=8 * all_experts * PACKED * tokens,
            transcendentals=0,
        ),
        name="mixer",
    )(picks, probs)


def mix_kernel(mix_ref, back_ref, *refs):
    out_ref = refs[-1]
    tokens = out_ref.shape[0]
    start = refs[0].shape[1] if len(refs) > 1 else 0
    half = back_ref.shape[1]
    both = jnp.dot(mix_ref[...], back_ref[...], preferred_element_type=jnp.float32)
    total = (both[: 2 * tokens] + both[2 * tokens :]).astype(jnp.bfloat16)
    if start:
        out_ref[:, :start] = refs[0][...]
    out_ref[:, start : start + half] = total[:tokens]
    out_ref[:, start + half :] = total[tokens:]


def mix_rows(mix, back, *ready):
    tokens = mix.shape[0] // 4
    width = 2 * back.shape[1] + sum(part.shape[1] for part in ready)
    operands = (mix, back, *ready)
    return pl.pallas_call(
        mix_kernel,
        out_shape=jax.ShapeDtypeStruct((tokens, width), jnp.bfloat16),
        grid=(1,),
        in_specs=[pl.BlockSpec(part.shape, lambda i: (0, 0)) for part in operands],
        out_specs=pl.BlockSpec((tokens, width), lambda i: (0, 0)),
        compiler_params=pltpu.CompilerParams(vmem_limit_bytes=24 << 20),
        cost_estimate=pl.CostEstimate(
            flops=2 * mix.shape[0] * mix.shape[1] * back.shape[1],
            bytes_accessed=2 * (mix.size + back.size + tokens * width),
            transcendentals=0,
        ),
        name="mix",
    )(*operands)


def source_ranks(ranks, rightward):
    me = lax.axis_index("rep")
    offsets = [0] + [-s for s in range(1, rightward + 1)] + list(range(1, ranks - rightward))
    return [lax.rem(me + (offset + ranks), ranks) for offset in offsets]


def piece_copies(rightward, piece_refs, whole, sem):
    rows = piece_refs[0].shape[0]
    copies = []
    for ref, source in zip(piece_refs, source_ranks(len(piece_refs), rightward)):
        place = whole.at[pl.ds(pl.multiple_of(source * rows, rows), rows), :]
        ref = ref.at[:, : whole.shape[1]]
        copies.append(pltpu.make_async_copy(ref, place, sem.at[len(copies)]))
    return copies


def early_copies(rightwards, ring_refs, whole, sems):
    rows, quarter = whole.shape[0] // len(ring_refs[0]), whole.shape[1] // 4
    copies = []
    for ring, (refs, rightward) in enumerate(zip(ring_refs, rightwards)):
        for i, (ref, source) in enumerate(zip(refs, source_ranks(len(refs), rightward))):
            for half in range(2):
                column = (2 * ring + half) * quarter
                place = whole.at[
                    pl.ds(pl.multiple_of(source * rows, rows), rows), column : column + quarter
                ]
                piece = ref.at[half * rows : (half + 1) * rows, ref.shape[1] - quarter :]
                copies.append(pltpu.make_async_copy(piece, place, sems.at[2 * ring + half, i]))
    return copies


def gated(rows, weight):
    both = jnp.dot(rows, weight, preferred_element_type=jnp.float32)
    half = both.shape[1] // 2
    gate, up = both[:, :half], both[:, half:]
    return (gate * (0.5 * jnp.tanh(0.5 * gate) + 0.5) * up).astype(jnp.bfloat16)


def gate_kernel(pieces, rightward, rows_ref, *refs):
    piece_refs, (unit_ref, whole, sem) = refs[:pieces], refs[pieces:]

    @pl.when(pl.program_id(0) == 0)
    def _():
        copies = piece_copies(rightward, piece_refs, whole, sem)
        for copy in copies:
            copy.start()
        for copy in copies:
            copy.wait()

    unit_ref[...] = gated(rows_ref[...], whole[...])


def gate_units(rows, pieces, rightward, columns):
    count, width = rows.shape
    depth = pieces[0].shape[0]
    block = 320
    return pl.pallas_call(
        functools.partial(gate_kernel, len(pieces), rightward),
        out_shape=jax.ShapeDtypeStruct((count, columns // 2), jnp.bfloat16),
        grid=(count // block,),
        in_specs=[pl.BlockSpec((block, width), lambda i: (i, 0))]
        + [pl.BlockSpec(memory_space=pl.ANY)] * len(pieces),
        out_specs=pl.BlockSpec((block, columns // 2), lambda i: (i, 0)),
        scratch_shapes=[
            pltpu.VMEM((depth * len(pieces), columns), jnp.bfloat16),
            pltpu.SemaphoreType.DMA((len(pieces),)),
        ],
        compiler_params=pltpu.CompilerParams(vmem_limit_bytes=VMEM_LIMIT),
        cost_estimate=pl.CostEstimate(
            flops=2 * count * width * columns,
            bytes_accessed=2 * (count * width + width * columns + count * columns // 2),
            transcendentals=count * columns // 2,
        ),
        name="gate_units",
    )(rows, *pieces)


def packed_rows(left, right):
    group, half = left.shape[0] // PAD, left.shape[1]
    left, right = left.reshape(group, PAD, half), right.reshape(group, PAD, half)
    last = left[:, MAIN:, :] + pltpu.roll(right[:, MAIN:, :], PAD - CAP, 1)
    packed = jnp.concatenate([left[:, :MAIN, :], right[:, :MAIN, :], last], axis=1)
    return packed.reshape(group * PACKED, half).astype(jnp.bfloat16)


def front_kernel(pieces, rightwards, rows_ref, ready_ref, *refs):
    first_refs, second_refs, refs = refs[:pieces], refs[pieces : 2 * pieces], refs[2 * pieces :]
    unit_ref, out_ref, gate_whole, down_whole, gate_sem, down_sems = refs

    @pl.when(pl.program_id(0) == 0)
    def _():
        copies = piece_copies(rightwards[1], second_refs, gate_whole, gate_sem)
        copies += early_copies(rightwards, (first_refs, second_refs), down_whole, down_sems)
        for copy in copies:
            copy.start()
        for copy in copies:
            copy.wait()

    unit = gated(rows_ref[...], gate_whole[...])
    unit_ref[...] = unit
    block = jnp.concatenate([ready_ref[...], unit], axis=1)
    total = jnp.dot(block, down_whole[...], preferred_element_type=jnp.float32)
    half = total.shape[1] // 2
    out_ref[...] = packed_rows(total[:, :half], total[:, half:])


def front(rows, ready, first_pieces, second_pieces, rightwards, early):
    count, width = rows.shape
    ranks = len(second_pieces)
    depth = second_pieces[0].shape[0]
    columns = second_pieces[0].shape[1] - early // 4
    group, unit_count = 8, columns // 2
    block = group * PAD
    return pl.pallas_call(
        functools.partial(front_kernel, ranks, rightwards),
        out_shape=(
            jax.ShapeDtypeStruct((count, unit_count), jnp.bfloat16),
            jax.ShapeDtypeStruct((count // PAD * PACKED, early // 2), jnp.bfloat16),
        ),
        grid=(count // block,),
        in_specs=[
            pl.BlockSpec((block, width), lambda i: (i, 0)),
            pl.BlockSpec((block, ready.shape[1]), lambda i: (i, 0)),
        ]
        + [pl.BlockSpec(memory_space=pl.ANY)] * (2 * ranks),
        out_specs=(
            pl.BlockSpec((block, unit_count), lambda i: (i, 0)),
            pl.BlockSpec((group * PACKED, early // 2), lambda i: (i, 0)),
        ),
        scratch_shapes=[
            pltpu.VMEM((depth * ranks, columns), jnp.bfloat16),
            pltpu.VMEM((depth // 2 * ranks, early), jnp.bfloat16),
            pltpu.SemaphoreType.DMA((ranks,)),
            pltpu.SemaphoreType.DMA((4, ranks)),
        ],
        compiler_params=pltpu.CompilerParams(vmem_limit_bytes=VMEM_LIMIT),
        cost_estimate=pl.CostEstimate(
            flops=2 * count * (width * columns + depth // 2 * ranks * early),
            bytes_accessed=2 * (count * width + width * columns + count * columns),
            transcendentals=count * unit_count,
        ),
        name="front",
    )(rows, ready, *first_pieces, *second_pieces)


def late_down_kernel(unit_count, pieces, rightwards, *refs):
    unit_refs, refs = refs[:unit_count], refs[unit_count:]
    piece_refs, (out_ref, whole, sems) = refs[:-3], refs[-3:]

    @pl.when(pl.program_id(0) == 0)
    def _():
        copies, column = [], 0
        for ring, rightward in enumerate(rightwards):
            refs_of = piece_refs[ring * pieces : (ring + 1) * pieces]
            columns = refs_of[0].shape[1]
            place = whole.at[:, column : column + columns]
            copies += piece_copies(rightward, refs_of, place, sems.at[ring])
            column += columns
        for copy in copies:
            copy.start()
        for copy in copies:
            copy.wait()

    block = jnp.concatenate([unit_ref[...] for unit_ref in unit_refs], axis=1)
    total = jnp.dot(block, whole[...], preferred_element_type=jnp.float32)
    half = total.shape[1] // 2
    out_ref[...] = packed_rows(total[:, :half], total[:, half:])


def late_down_rows(units, rings, rightwards):
    count, pieces = units[0].shape[0], len(rings[0])
    depth = rings[0][0].shape[0] * pieces
    columns = sum(ring[0].shape[1] for ring in rings)
    group, half = 8, columns // 2
    return pl.pallas_call(
        functools.partial(late_down_kernel, len(units), pieces, rightwards),
        out_shape=jax.ShapeDtypeStruct((count // PAD * PACKED, half), jnp.bfloat16),
        grid=(count // PAD // group,),
        in_specs=[
            pl.BlockSpec((group * PAD, part.shape[1]), lambda i: (i, 0)) for part in units
        ]
        + [pl.BlockSpec(memory_space=pl.ANY)] * (pieces * len(rings)),
        out_specs=pl.BlockSpec((group * PACKED, half), lambda i: (i, 0)),
        scratch_shapes=[
            pltpu.VMEM((depth, columns), jnp.bfloat16),
            pltpu.SemaphoreType.DMA((len(rings), pieces)),
        ],
        compiler_params=pltpu.CompilerParams(vmem_limit_bytes=VMEM_LIMIT),
        cost_estimate=pl.CostEstimate(
            flops=4 * count * depth * half,
            bytes_accessed=2 * depth * (count + 2 * half) + 4 * count * half,
            transcendentals=0,
        ),
        name="late_down_rows",
    )(*units, *[piece for ring in rings for piece in ring])


class Rings:
    def __init__(self, ranks, window):
        self.ranks, self.window = ranks, window
        self.pieces = {}
        self.sent = {"right": [], "left": []}

    def add(self, name, piece):
        self.pieces[name] = {"right": [piece], "left": [piece]}

    def hop(self, way, name, level):
        chain = self.pieces[name][way]
        before = level - self.window
        waits = [sent[before] for sent in self.sent.values() if before >= 0]
        waits = [piece for piece in waits if piece is not None]
        piece, *_ = lax.optimization_barrier((chain[-1], *waits))
        turn = 1 if way == "right" else -1
        pairs = [(i, (i + turn) % self.ranks) for i in range(self.ranks)]
        chain.append(lax.ppermute(piece, "rep", pairs))
        return chain[-1]

    def hops(self, right, left):
        for step in range(max(len(right), len(left))):
            level = len(self.sent["right"])
            names = {"right": right[step : step + 1], "left": left[step : step + 1]}
            arrived = {way: self.hop(way, name, level) for way, name in names.items() if name}
            for way in names:
                self.sent[way].append(arrived.get(way))

    def all(self, name):
        chains = self.pieces[name]
        return chains["right"] + chains["left"][1:]

    def rightward(self, name):
        return len(self.pieces[name]["right"]) - 1


def per_device(hidden_states, routes, gate_prob, gate_up, down):
    groups = lax.axis_size("tok")
    ranks = lax.axis_size("rep")
    width = hidden_states.shape[2]
    unit_count = gate_up.shape[2] // 2
    all_experts = groups * gate_up.shape[0]
    gate_up, down, rows = gate_up[0], down[0], hidden_states[0]

    def ring_piece(ring):
        start, stop = ring * unit_count // 2, (ring + 1) * unit_count // 2
        quarters = [
            down[:, (2 * ring + half) * EARLY // 4 : (2 * ring + half + 1) * EARLY // 4]
            for half in range(2)
        ]
        columns = [
            gate_up[:, start:stop],
            gate_up[:, unit_count + start : unit_count + stop],
            jnp.concatenate(quarters, axis=0),
        ]
        return jnp.concatenate([part.astype(jnp.bfloat16) for part in columns], axis=1)

    def down_piece(start, stop):
        return down[:, start:stop].astype(jnp.bfloat16)

    rings = Rings(ranks, WINDOW)
    rings.add("A", ring_piece(0))
    rings.add("B", ring_piece(1))
    rings.hops(*ORDER)
    middle = (EARLY + width) // 2
    rings.add("e", down_piece(EARLY, middle))
    rings.add("f", down_piece(middle, width))
    rings.hops(*LATE_ORDER)

    picks, probs = routes[0].T, gate_prob[0].T
    send = dispatch(picks, rows, all_experts)
    arrived = lax.all_to_all(
        send.reshape(groups, PAD, width), "tok", split_axis=0, concat_axis=0, tiled=True
    ).reshape(groups * PAD, width)
    waits = [sent[0] for sent in rings.sent.values()]
    picks, *_ = lax.optimization_barrier((picks, *waits))
    mix = mixer(picks, probs, all_experts)
    arrived, mix = lax.optimization_barrier((arrived, mix))

    units = [gate_units(arrived, rings.all("A"), rings.rightward("A"), unit_count)]
    second, sent = front(
        arrived,
        units[0],
        rings.all("A"),
        rings.all("B"),
        [rings.rightward("A"), rings.rightward("B")],
        EARLY,
    )
    units.append(second)
    ready = ()
    for part in range(2):
        if part:
            sent = late_down_rows(
                units, [rings.all(name) for name in "ef"], [rings.rightward(name) for name in "ef"]
            )
        half = sent.shape[1]
        back = lax.all_to_all(
            sent.reshape(groups, PACKED, half), "tok", split_axis=0, concat_axis=0, tiled=True
        ).reshape(groups * PACKED, half)
        ready = (mix_rows(mix, back, *ready),)
    return ready[0][None]


def solution(mesh):
    return jax.shard_map(
        per_device,
        mesh=mesh,
        in_specs=(
            P("rep", "tok", None),
            P("rep", "tok", None),
            P("rep", "tok", None),
            P("tok", "rep", None),
            P("tok", "rep", None),
        ),
        out_specs=P("rep", "tok", None),
        check_vma=False,
    )
```

```python
import functools

import jax
import jax.numpy as jnp
from jax import lax
from jax.experimental import pallas as pl
from jax.experimental.pallas import tpu as pltpu
from jax.sharding import PartitionSpec as P

CAP = 36
PAD = 40
MAIN = 32
PACKED = 72
NONE = 200.0
EARLY = 1024
WINDOW = 2
MIXER_FLOPS = 40 * 10**9
ORDER = ("ABABAAB", "ABABABB")
LATE_ORDER = ("efefefe", "efefeff")
VMEM_LIMIT = 56 << 20


def slots_of(picks, experts):
    count, tokens = experts.shape[0], picks.shape[1]
    named = jnp.zeros((count, tokens), jnp.float32)
    for k in range(picks.shape[0]):
        named = named + (picks[k : k + 1, :] == experts).astype(jnp.float32)
    before = lax.broadcasted_iota(jnp.int32, (tokens, tokens), 0)
    after = lax.broadcasted_iota(jnp.int32, (tokens, tokens), 1)
    earlier = (before < after).astype(jnp.bfloat16)
    slot = jnp.dot(named.astype(jnp.bfloat16), earlier, preferred_element_type=jnp.float32)
    return jnp.where(named > 0.0, slot, NONE)


def dispatch_kernel(picks_ref, rows_ref, send_ref):
    tokens = picks_ref.shape[1]
    group = send_ref.shape[0] // PAD
    experts = pl.program_id(0) * group + lax.broadcasted_iota(jnp.int32, (group, tokens), 0)
    slot = slots_of(picks_ref[...], experts)
    place = lax.broadcasted_iota(jnp.int32, (group, PAD, tokens), 1).astype(jnp.float32)
    chosen = (slot[:, None, :] == place).astype(jnp.float32)
    chosen = chosen.reshape(group * PAD, tokens).astype(jnp.bfloat16)
    send_ref[...] = jnp.dot(chosen, rows_ref[...], preferred_element_type=jnp.float32).astype(
        jnp.bfloat16
    )


def dispatch(picks, rows, all_experts):
    top, tokens = picks.shape
    width = rows.shape[1]
    group = 16
    return pl.pallas_call(
        dispatch_kernel,
        out_shape=jax.ShapeDtypeStruct((all_experts * PAD, width), jnp.bfloat16),
        grid=(all_experts // group,),
        in_specs=[
            pl.BlockSpec((top, tokens), lambda i: (0, 0)),
            pl.BlockSpec((tokens, width), lambda i: (0, 0)),
        ],
        out_specs=pl.BlockSpec((group * PAD, width), lambda i: (i, 0)),
        cost_estimate=pl.CostEstimate(
            flops=2 * all_experts * PAD * tokens * width,
            bytes_accessed=2 * width * (tokens + all_experts * PAD),
            transcendentals=0,
        ),
        compiler_params=pltpu.CompilerParams(vmem_limit_bytes=VMEM_LIMIT),
        name="dispatch",
    )(picks, rows)


def mixer_kernel(picks_ref, probs_ref, mix_ref):
    tokens = picks_ref.shape[1]
    group = mix_ref.shape[1] // PACKED
    experts = pl.program_id(0) * group + lax.broadcasted_iota(jnp.int32, (group, tokens), 0)
    slot = slots_of(picks_ref[...], experts)
    weight = jnp.zeros((group, tokens), jnp.float32)
    for k in range(picks_ref.shape[0]):
        weight = weight + jnp.where(
            picks_ref[k : k + 1, :] == experts, probs_ref[k : k + 1, :], 0.0
        )
    first = jnp.where(slot < MAIN, slot, slot + MAIN)
    second = jnp.where(slot < MAIN, slot + MAIN, slot + CAP)
    row = jnp.concatenate([first, second], axis=1)
    weight = jnp.concatenate([weight, weight], axis=1)
    place = lax.broadcasted_iota(jnp.int32, (group, PACKED, 2 * tokens), 1).astype(jnp.float32)
    spread = jnp.where(row[:, None, :] == place, weight[:, None, :], 0.0)
    spread = spread.reshape(group * PACKED, 2 * tokens).T
    high = spread.astype(jnp.bfloat16)
    mix_ref[: 2 * tokens, :] = high
    mix_ref[2 * tokens :, :] = (spread - high.astype(jnp.float32)).astype(jnp.bfloat16)


def mixer(picks, probs, all_experts):
    top, tokens = picks.shape
    group = 16
    return pl.pallas_call(
        mixer_kernel,
        out_shape=jax.ShapeDtypeStruct((4 * tokens, all_experts * PACKED), jnp.bfloat16),
        grid=(all_experts // group,),
        in_specs=[
            pl.BlockSpec((top, tokens), lambda i: (0, 0)),
            pl.BlockSpec((top, tokens), lambda i: (0, 0)),
        ],
        out_specs=pl.BlockSpec((4 * tokens, group * PACKED), lambda i: (0, i)),
        compiler_params=pltpu.CompilerParams(vmem_limit_bytes=32 << 20),
        cost_estimate=pl.CostEstimate(
            flops=MIXER_FLOPS,
            bytes_accessed=8 * all_experts * PACKED * tokens,
            transcendentals=0,
        ),
        name="mixer",
    )(picks, probs)


def mix_kernel(mix_ref, back_ref, *refs):
    out_ref = refs[-1]
    tokens = out_ref.shape[0]
    start = refs[0].shape[1] if len(refs) > 1 else 0
    half = back_ref.shape[1]
    both = jnp.dot(mix_ref[...], back_ref[...], preferred_element_type=jnp.float32)
    total = (both[: 2 * tokens] + both[2 * tokens :]).astype(jnp.bfloat16)
    if start:
        out_ref[:, :start] = refs[0][...]
    out_ref[:, start : start + half] = total[:tokens]
    out_ref[:, start + half :] = total[tokens:]


def mix_rows(mix, back, *ready):
    tokens = mix.shape[0] // 4
    width = 2 * back.shape[1] + sum(part.shape[1] for part in ready)
    operands = (mix, back, *ready)
    return pl.pallas_call(
        mix_kernel,
        out_shape=jax.ShapeDtypeStruct((tokens, width), jnp.bfloat16),
        grid=(1,),
        in_specs=[pl.BlockSpec(part.shape, lambda i: (0, 0)) for part in operands],
        out_specs=pl.BlockSpec((tokens, width), lambda i: (0, 0)),
        compiler_params=pltpu.CompilerParams(vmem_limit_bytes=24 << 20),
        cost_estimate=pl.CostEstimate(
            flops=2 * mix.shape[0] * mix.shape[1] * back.shape[1],
            bytes_accessed=2 * (mix.size + back.size + tokens * width),
            transcendentals=0,
        ),
        name="mix",
    )(*operands)


def source_ranks(ranks, rightward):
    me = lax.axis_index("rep")
    offsets = [0] + [-s for s in range(1, rightward + 1)] + list(range(1, ranks - rightward))
    return [lax.rem(me + (offset + ranks), ranks) for offset in offsets]


def piece_copies(rightward, piece_refs, whole, sem):
    rows = piece_refs[0].shape[0]
    copies = []
    for ref, source in zip(piece_refs, source_ranks(len(piece_refs), rightward)):
        place = whole.at[pl.ds(pl.multiple_of(source * rows, rows), rows), :]
        ref = ref.at[:, : whole.shape[1]]
        copies.append(pltpu.make_async_copy(ref, place, sem.at[len(copies)]))
    return copies


def early_copies(rightwards, ring_refs, whole, sems):
    rows, quarter = whole.shape[0] // len(ring_refs[0]), whole.shape[1] // 4
    copies = []
    for ring, (refs, rightward) in enumerate(zip(ring_refs, rightwards)):
        for i, (ref, source) in enumerate(zip(refs, source_ranks(len(refs), rightward))):
            for half in range(2):
                column = (2 * ring + half) * quarter
                place = whole.at[
                    pl.ds(pl.multiple_of(source * rows, rows), rows), column : column + quarter
                ]
                piece = ref.at[half * rows : (half + 1) * rows, ref.shape[1] - quarter :]
                copies.append(pltpu.make_async_copy(piece, place, sems.at[2 * ring + half, i]))
    return copies


def gated(rows, weight):
    both = jnp.dot(rows, weight, preferred_element_type=jnp.float32)
    half = both.shape[1] // 2
    gate, up = both[:, :half], both[:, half:]
    return (gate * (0.5 * jnp.tanh(0.5 * gate) + 0.5) * up).astype(jnp.bfloat16)


def gate_kernel(pieces, rightward, rows_ref, *refs):
    piece_refs, (unit_ref, whole, sem) = refs[:pieces], refs[pieces:]

    @pl.when(pl.program_id(0) == 0)
    def _():
        copies = piece_copies(rightward, piece_refs, whole, sem)
        for copy in copies:
            copy.start()
        for copy in copies:
            copy.wait()

    unit_ref[...] = gated(rows_ref[...], whole[...])


def gate_units(rows, pieces, rightward, columns):
    count, width = rows.shape
    depth = pieces[0].shape[0]
    block = 320
    return pl.pallas_call(
        functools.partial(gate_kernel, len(pieces), rightward),
        out_shape=jax.ShapeDtypeStruct((count, columns // 2), jnp.bfloat16),
        grid=(count // block,),
        in_specs=[pl.BlockSpec((block, width), lambda i: (i, 0))]
        + [pl.BlockSpec(memory_space=pl.ANY)] * len(pieces),
        out_specs=pl.BlockSpec((block, columns // 2), lambda i: (i, 0)),
        scratch_shapes=[
            pltpu.VMEM((depth * len(pieces), columns), jnp.bfloat16),
            pltpu.SemaphoreType.DMA((len(pieces),)),
        ],
        compiler_params=pltpu.CompilerParams(vmem_limit_bytes=VMEM_LIMIT),
        cost_estimate=pl.CostEstimate(
            flops=2 * count * width * columns,
            bytes_accessed=2 * (count * width + width * columns + count * columns // 2),
            transcendentals=count * columns // 2,
        ),
        name="gate_units",
    )(rows, *pieces)


def packed_rows(left, right):
    group, half = left.shape[0] // PAD, left.shape[1]
    left, right = left.reshape(group, PAD, half), right.reshape(group, PAD, half)
    last = left[:, MAIN:, :] + pltpu.roll(right[:, MAIN:, :], PAD - CAP, 1)
    packed = jnp.concatenate([left[:, :MAIN, :], right[:, :MAIN, :], last], axis=1)
    return packed.reshape(group * PACKED, half).astype(jnp.bfloat16)


def front_kernel(pieces, rightwards, rows_ref, ready_ref, *refs):
    first_refs, second_refs, refs = refs[:pieces], refs[pieces : 2 * pieces], refs[2 * pieces :]
    unit_ref, out_ref, gate_whole, down_whole, gate_sem, down_sems = refs

    @pl.when(pl.program_id(0) == 0)
    def _():
        copies = piece_copies(rightwards[1], second_refs, gate_whole, gate_sem)
        copies += early_copies(rightwards, (first_refs, second_refs), down_whole, down_sems)
        for copy in copies:
            copy.start()
        for copy in copies:
            copy.wait()

    unit = gated(rows_ref[...], gate_whole[...])
    unit_ref[...] = unit
    block = jnp.concatenate([ready_ref[...], unit], axis=1)
    total = jnp.dot(block, down_whole[...], preferred_element_type=jnp.float32)
    half = total.shape[1] // 2
    out_ref[...] = packed_rows(total[:, :half], total[:, half:])


def front(rows, ready, first_pieces, second_pieces, rightwards, early):
    count, width = rows.shape
    ranks = len(second_pieces)
    depth = second_pieces[0].shape[0]
    columns = second_pieces[0].shape[1] - early // 4
    group, unit_count = 8, columns // 2
    block = group * PAD
    return pl.pallas_call(
        functools.partial(front_kernel, ranks, rightwards),
        out_shape=(
            jax.ShapeDtypeStruct((count, unit_count), jnp.bfloat16),
            jax.ShapeDtypeStruct((count // PAD * PACKED, early // 2), jnp.bfloat16),
        ),
        grid=(count // block,),
        in_specs=[
            pl.BlockSpec((block, width), lambda i: (i, 0)),
            pl.BlockSpec((block, ready.shape[1]), lambda i: (i, 0)),
        ]
        + [pl.BlockSpec(memory_space=pl.ANY)] * (2 * ranks),
        out_specs=(
            pl.BlockSpec((block, unit_count), lambda i: (i, 0)),
            pl.BlockSpec((group * PACKED, early // 2), lambda i: (i, 0)),
        ),
        scratch_shapes=[
            pltpu.VMEM((depth * ranks, columns), jnp.bfloat16),
            pltpu.VMEM((depth // 2 * ranks, early), jnp.bfloat16),
            pltpu.SemaphoreType.DMA((ranks,)),
            pltpu.SemaphoreType.DMA((4, ranks)),
        ],
        compiler_params=pltpu.CompilerParams(vmem_limit_bytes=VMEM_LIMIT),
        cost_estimate=pl.CostEstimate(
            flops=2 * count * (width * columns + depth // 2 * ranks * early),
            bytes_accessed=2 * (count * width + width * columns + count * columns),
            transcendentals=count * unit_count,
        ),
        name="front",
    )(rows, ready, *first_pieces, *second_pieces)


def late_down_kernel(unit_count, pieces, rightwards, *refs):
    unit_refs, refs = refs[:unit_count], refs[unit_count:]
    piece_refs, (out_ref, whole, sems) = refs[:-3], refs[-3:]

    @pl.when(pl.program_id(0) == 0)
    def _():
        copies, column = [], 0
        for ring, rightward in enumerate(rightwards):
            refs_of = piece_refs[ring * pieces : (ring + 1) * pieces]
            columns = refs_of[0].shape[1]
            place = whole.at[:, column : column + columns]
            copies += piece_copies(rightward, refs_of, place, sems.at[ring])
            column += columns
        for copy in copies:
            copy.start()
        for copy in copies:
            copy.wait()

    block = jnp.concatenate([unit_ref[...] for unit_ref in unit_refs], axis=1)
    total = jnp.dot(block, whole[...], preferred_element_type=jnp.float32)
    half = total.shape[1] // 2
    out_ref[...] = packed_rows(total[:, :half], total[:, half:])


def late_down_rows(units, rings, rightwards):
    count, pieces = units[0].shape[0], len(rings[0])
    depth = rings[0][0].shape[0] * pieces
    columns = sum(ring[0].shape[1] for ring in rings)
    group, half = 8, columns // 2
    return pl.pallas_call(
        functools.partial(late_down_kernel, len(units), pieces, rightwards),
        out_shape=jax.ShapeDtypeStruct((count // PAD * PACKED, half), jnp.bfloat16),
        grid=(count // PAD // group,),
        in_specs=[
            pl.BlockSpec((group * PAD, part.shape[1]), lambda i: (i, 0)) for part in units
        ]
        + [pl.BlockSpec(memory_space=pl.ANY)] * (pieces * len(rings)),
        out_specs=pl.BlockSpec((group * PACKED, half), lambda i: (i, 0)),
        scratch_shapes=[
            pltpu.VMEM((depth, columns), jnp.bfloat16),
            pltpu.SemaphoreType.DMA((len(rings), pieces)),
        ],
        compiler_params=pltpu.CompilerParams(vmem_limit_bytes=VMEM_LIMIT),
        cost_estimate=pl.CostEstimate(
            flops=4 * count * depth * half,
            bytes_accessed=2 * depth * (count + 2 * half) + 4 * count * half,
            transcendentals=0,
        ),
        name="late_down_rows",
    )(*units, *[piece for ring in rings for piece in ring])


class Rings:
    def __init__(self, ranks, window):
        self.ranks, self.window = ranks, window
        self.pieces = {}
        self.sent = {"right": [], "left": []}

    def add(self, name, piece):
        self.pieces[name] = {"right": [piece], "left": [piece]}

    def hop(self, way, name, level):
        chain = self.pieces[name][way]
        before = level - self.window
        waits = [sent[before] for sent in self.sent.values() if before >= 0]
        waits = [piece for piece in waits if piece is not None]
        piece, *_ = lax.optimization_barrier((chain[-1], *waits))
        turn = 1 if way == "right" else -1
        pairs = [(i, (i + turn) % self.ranks) for i in range(self.ranks)]
        chain.append(lax.ppermute(piece, "rep", pairs))
        return chain[-1]

    def hops(self, right, left):
        for step in range(max(len(right), len(left))):
            level = len(self.sent["right"])
            names = {"right": right[step : step + 1], "left": left[step : step + 1]}
            arrived = {way: self.hop(way, name, level) for way, name in names.items() if name}
            for way in names:
                self.sent[way].append(arrived.get(way))

    def all(self, name):
        chains = self.pieces[name]
        return chains["right"] + chains["left"][1:]

    def rightward(self, name):
        return len(self.pieces[name]["right"]) - 1


def per_device(hidden_states, routes, gate_prob, gate_up, down):
    groups = lax.axis_size("tok")
    ranks = lax.axis_size("rep")
    width = hidden_states.shape[2]
    unit_count = gate_up.shape[2] // 2
    all_experts = groups * gate_up.shape[0]
    gate_up, down, rows = gate_up[0], down[0], hidden_states[0]

    def ring_piece(ring):
        start, stop = ring * unit_count // 2, (ring + 1) * unit_count // 2
        quarters = [
            down[:, (2 * ring + half) * EARLY // 4 : (2 * ring + half + 1) * EARLY // 4]
            for half in range(2)
        ]
        columns = [
            gate_up[:, start:stop],
            gate_up[:, unit_count + start : unit_count + stop],
            jnp.concatenate(quarters, axis=0),
        ]
        return jnp.concatenate([part.astype(jnp.bfloat16) for part in columns], axis=1)

    def down_piece(start, stop):
        return down[:, start:stop].astype(jnp.bfloat16)

    rings = Rings(ranks, WINDOW)
    rings.add("A", ring_piece(0))
    rings.add("B", ring_piece(1))
    rings.hops(*ORDER)
    middle = (EARLY + width) // 2
    rings.add("e", down_piece(EARLY, middle))
    rings.add("f", down_piece(middle, width))
    rings.hops(*LATE_ORDER)

    picks, probs = routes[0].T, gate_prob[0].T
    send = dispatch(picks, rows, all_experts)
    arrived = lax.all_to_all(
        send.reshape(groups, PAD, width), "tok", split_axis=0, concat_axis=0, tiled=True
    ).reshape(groups * PAD, width)
    waits = [sent[0] for sent in rings.sent.values()]
    picks, *_ = lax.optimization_barrier((picks, *waits))
    mix = mixer(picks, probs, all_experts)
    arrived, mix = lax.optimization_barrier((arrived, mix))

    units = [gate_units(arrived, rings.all("A"), rings.rightward("A"), unit_count)]
    second, sent = front(
        arrived,
        units[0],
        rings.all("A"),
        rings.all("B"),
        [rings.rightward("A"), rings.rightward("B")],
        EARLY,
    )
    units.append(second)
    ready = ()
    for part in range(2):
        if part:
            sent = late_down_rows(
                units, [rings.all(name) for name in "ef"], [rings.rightward(name) for name in "ef"]
            )
        half = sent.shape[1]
        back = lax.all_to_all(
            sent.reshape(groups, PACKED, half), "tok", split_axis=0, concat_axis=0, tiled=True
        ).reshape(groups * PACKED, half)
        ready = (mix_rows(mix, back, *ready),)
    return ready[0][None]


def solution(mesh):
    return jax.shard_map(
        per_device,
        mesh=mesh,
        in_specs=(
            P("rep", "tok", None),
            P("rep", "tok", None),
            P("rep", "tok", None),
            P("tok", "rep", None),
            P("tok", "rep", None),
        ),
        out_specs=P("rep", "tok", None),
        check_vma=False,
    )
```
